32 devices in a mesh: dp: 2 (over x), row: 4 (over z), col: 4 (over y, core).
Axes of the slice: x: 2, y: 2, z: 4, core: 2. Of those that a mesh axis runs over, the one named last changes fastest.
Arguments:
- stash_codes: int32 [1024, 4096], P(('dp', 'col'), 'row'), may hold values from 0 to 3
- stash_scales: int32 [1024, 32], P(('dp', 'col'), 'row'), may hold values from 1 to 8
- pad_mask: int32 [1024], P(('dp', 'col')), may hold values 0 or 1
- cotangent: bfloat16 [1024, 4096], P(('dp', 'col'), 'row'), may hold values from -3 to 3
- w_gate: bfloat16 [4096, 10240], P('row', 'col'), may hold values from -0.09375 to 0.09375
- w_up: bfloat16 [4096, 10240], P('row', 'col'), may hold values from -0.09375 to 0.09375
- w_out: bfloat16 [4096, 10240], P('row', 'col'), may hold values from -0.09375 to 0.09375
Outputs:
- input_grad: float32 [1024, 4096], P(('dp', 'col'), 'row')
- gate_weight_grad: float32 [4096, 10240], P('row', 'col')
- up_weight_grad: float32 [4096, 10240], P('row', 'col')
- out_weight_grad: float32 [4096, 10240], P('row', 'col')
The draws below stay inside these ranges and needn't reach their ends.
All inputs are finite; a program needn't handle non-finite values. No bound on the sum of `pad_mask` on one device may be relied on, other than what follows from the above.
Results may differ from the reference program's by a relative error of at most 0.0029.
Values may be sent and summed in bfloat16 or wider, within the bound.
No kernel may reach another device: no remote copies, remote signals or barrier semaphores. Data moves between devices by JAX's collectives and lax.ppermute only.
A program may use at most 192 MiB of HBM per device.

```python
import jax
import jax.numpy as jnp

D = 4096
FF = 10240
QBLOCK = 128
TOKENS = 1024


def place_ends(result, stream_key, least, high):
    longest = result.shape.index(max(result.shape))
    spots = []
    for shift in (0, 1):
        where = [jax.random.randint(jax.random.fold_in(stream_key, axis), (), 0, length) for axis, length in enumerate(result.shape)]
        where[longest] = (where[longest] + shift) % result.shape[longest]
        spots.append(tuple(where))
    return result.at[spots[0]].set(least).at[spots[1]].set(high)


def level_of(own_key, dims, split, least, top_value):
    factor_of, own = 1.0, jax.random.fold_in(own_key, 6)
    for axis_at, blocks in split:
        draws = jnp.exp(jax.random.uniform(jax.random.fold_in(own, axis_at), (blocks,), jnp.float32, least / len(split), top_value / len(split)))
        factor_of = factor_of * jnp.repeat(draws, dims[axis_at] // blocks).reshape([-1 if axis == axis_at else 1 for axis in range(len(dims))])
    return factor_of


def scatter_about(stream_key, extent, scale, most, cuts=(), kind=jnp.bfloat16):
    entries = jax.random.normal(stream_key, extent, jnp.float32) * scale
    if len(cuts) > 0:
        entries = level_of(stream_key, extent, cuts, -0.22, 0.18) * entries
    return jnp.clip(entries, min=-most, max=most).astype(kind)


def setup_inputs(seed: int = 0) -> dict:
    streams_of = jax.random.split(jax.random.key(seed), 8)
    stash_codes = place_ends(jax.random.randint(streams_of[0], (TOKENS, D), 0, 4), jax.random.fold_in(streams_of[0], 1), 0, 3).astype(jnp.int32)
    stash_scales = place_ends(jax.random.randint(streams_of[1], (TOKENS, D // QBLOCK), 1, 9), jax.random.fold_in(streams_of[1], 1), 1, 8).astype(jnp.int32)
    pad_mask = place_ends((jax.random.randint(streams_of[2], (TOKENS,), 0, 4) < 3).astype(jnp.int32), jax.random.fold_in(streams_of[2], 1), 0, 1)
    cotangent = scatter_about(streams_of[3], (TOKENS, D), 0.5, 3.0, ((0, 8), (1, 4)))
    w_gate = scatter_about(streams_of[4], (D, FF), D ** -0.5, 0.09375, ((0, 4), (1, 4)))
    w_up = scatter_about(streams_of[5], (D, FF), D ** -0.5, 0.09375, ((0, 4), (1, 4)))
    w_out = scatter_about(streams_of[6], (D, FF), D ** -0.5, 0.09375, ((0, 4), (1, 4)))
    return dict(stash_codes=stash_codes, stash_scales=stash_scales, pad_mask=pad_mask, cotangent=cotangent, w_gate=w_gate, w_up=w_up, w_out=w_out)


root_term = 0.7978845608028654
cubic_term = 0.044715


def gelu_pair(values):
    inside = root_term * (values + cubic_term * values * values * values)
    tangent = jnp.tanh(inside)
    activated = 0.5 * values * (1.0 + tangent)
    derivative = 0.5 * (1.0 + tangent) + 0.5 * values * (1.0 - tangent * tangent) * root_term * (1.0 + 3.0 * cubic_term * values * values)
    return activated, derivative


def unpack_stash(stash_codes, stash_scales):
    blocks = stash_scales.shape[1]
    block_width = stash_codes.shape[1] // blocks
    levels = (2 * stash_codes - 3).astype(jnp.float32).reshape(stash_codes.shape[0], blocks, block_width)
    scaled = levels * stash_scales.astype(jnp.float32)[:, :, None] / 16.0
    return scaled.reshape(stash_codes.shape).astype(jnp.bfloat16)


def reference(stash_codes, stash_scales, pad_mask, cotangent, w_gate, w_up, w_out):
    stashed = unpack_stash(stash_codes, stash_scales)
    live_grad = (cotangent.astype(jnp.float32) * pad_mask.astype(jnp.float32)[:, None]).astype(jnp.bfloat16)
    gate_pre = jnp.dot(stashed, w_gate, preferred_element_type=jnp.float32)
    up_part = jnp.dot(stashed, w_up, preferred_element_type=jnp.float32)
    back_grad = jnp.dot(live_grad, w_out, preferred_element_type=jnp.float32)
    activated, derivative = gelu_pair(gate_pre)
    hidden = (activated * up_part).astype(jnp.bfloat16)
    gate_grad = (back_grad * up_part * derivative).astype(jnp.bfloat16)
    up_grad = (back_grad * activated).astype(jnp.bfloat16)
    input_grad = jnp.dot(gate_grad, w_gate.T, preferred_element_type=jnp.float32) + jnp.dot(up_grad, w_up.T, preferred_element_type=jnp.float32)
    gate_weight_grad = jnp.dot(stashed.T, gate_grad, preferred_element_type=jnp.float32)
    up_weight_grad = jnp.dot(stashed.T, up_grad, preferred_element_type=jnp.float32)
    out_weight_grad = jnp.dot(live_grad.T, hidden, preferred_element_type=jnp.float32)
    return input_grad, gate_weight_grad, up_weight_grad, out_weight_grad
```

```python
import functools

import jax
import jax.numpy as jnp
from jax import lax
from jax.experimental import pallas as pl
from jax.experimental.pallas import tpu as pltpu
from jax.sharding import PartitionSpec as P

root_term = 0.7978845608028654
cubic_term = 0.044715
lanes = 128
stash_bound = 1.5
half_range = 32000.0
shares = (1, 3, 4, 2)


def gelu_pair(values):
    inside = root_term * (values + cubic_term * values * values * values)
    tangent = jnp.tanh(inside)
    activated = 0.5 * values * (1.0 + tangent)
    derivative = 0.5 * (1.0 + tangent) + 0.5 * values * (1.0 - tangent * tangent) * root_term * (
        1.0 + 3.0 * cubic_term * values * values
    )
    return (activated, derivative)


def unpack_stash(stash_codes, stash_scales):
    blocks = stash_scales.shape[1]
    block_width = stash_codes.shape[1] // blocks
    levels = (
        (2 * stash_codes - 3).astype(jnp.float32).reshape(stash_codes.shape[0], blocks, block_width)
    )
    scaled = levels * stash_scales.astype(jnp.float32)[:, :, None] / 16.0
    return scaled.reshape(stash_codes.shape).astype(jnp.bfloat16)


def block_of(width):
    return 256 if width % 256 == 0 else lanes


def params(mib=48):
    return pltpu.CompilerParams(vmem_limit_bytes=mib * 1024 * 1024)


def project_kernel(scale_ref, x_ref, g_ref, wg_ref, wu_ref, wo_ref, p_ref):
    for at, (left, right) in enumerate(((x_ref, wg_ref), (x_ref, wu_ref), (g_ref, wo_ref))):
        part = jnp.dot(left[...], right[...], preferred_element_type=jnp.float32)
        p_ref[at] = part * scale_ref[at]


def project(scale, x, g, wg, wu, wo, start, width):
    tokens, depth = x.shape
    step = block_of(width)
    first = start // step
    whole = pl.BlockSpec((tokens, depth), lambda j: (0, 0), pipeline_mode=pl.Buffered(1))
    columns = pl.BlockSpec((depth, step), lambda j: (0, first + j))
    return pl.pallas_call(
        project_kernel,
        grid=(width // step,),
        in_specs=[pl.BlockSpec(memory_space=pltpu.SMEM), whole, whole, columns, columns, columns],
        out_specs=pl.BlockSpec((3, tokens, step), lambda j: (0, 0, j)),
        out_shape=jax.ShapeDtypeStruct((3, tokens, width), jnp.float32),
        compiler_params=params(),
        cost_estimate=pl.CostEstimate(
            flops=6 * tokens * depth * width,
            bytes_accessed=4 * tokens * depth + 6 * depth * width + 12 * tokens * width,
            transcendentals=0,
        ),
        name="project",
    )(scale, x, g, wg, wu, wo)


def activate(inverse, p, recv_c, recv_b):
    unit = recv_b.shape[1]
    arrived = recv_c[:, :unit].astype(jnp.float32) + recv_b.astype(jnp.float32)
    gate_pre, up_part, back_grad = (p[:, :unit] + arrived) * inverse[:, None, None]
    activated, derivative = gelu_pair(gate_pre)
    return jnp.stack(
        [
            (back_grad * up_part * derivative).astype(jnp.bfloat16),
            (back_grad * activated).astype(jnp.bfloat16),
            (activated * up_part).astype(jnp.bfloat16),
        ]
    )


def weight_kernel(count, xt_ref, gt_ref, *refs):
    pieces, outs = refs[:count], refs[-3:]
    for at in range(3):
        left = gt_ref if at == 2 else xt_ref
        total, begin = None, 0
        for piece in pieces:
            rows = piece.shape[1]
            term = jnp.dot(
                left[:, begin : begin + rows], piece[at], preferred_element_type=jnp.float32
            )
            total = term if total is None else total + term
            begin += rows
        outs[at][...] = total


def weight_grads(xt, gt, pieces, held, start, width, full):
    depth, tokens = xt.shape
    step = block_of(width)
    first = start // step
    count = len(pieces)
    whole = pl.BlockSpec((depth, tokens), lambda j: (0, 0), pipeline_mode=pl.Buffered(1))
    specs = [pl.BlockSpec((3, a.shape[1], step), lambda j: (0, 0, j)) for a in pieces]
    return pl.pallas_call(
        functools.partial(weight_kernel, count),
        grid=(width // step,),
        in_specs=[whole, whole, *specs] + [pl.BlockSpec(memory_space=pl.ANY)] * len(held),
        out_specs=[pl.BlockSpec((depth, step), lambda j: (0, first + j))] * 3,
        out_shape=[jax.ShapeDtypeStruct((depth, full), jnp.float32)] * 3,
        input_output_aliases={2 + count + i: i for i in range(len(held))},
        compiler_params=params(),
        cost_estimate=pl.CostEstimate(
            flops=6 * tokens * depth * width,
            bytes_accessed=4 * tokens * depth + 6 * tokens * width + 12 * depth * width,
            transcendentals=0,
        ),
        name="weight_grads",
    )(xt, gt, *pieces, *held)


def input_kernel(started, pair_ref, far_ref, wg_ref, wu_ref, *refs):
    out_ref = refs[-1]
    half = pair_ref.shape[1]
    first = pl.program_id(0) == 0
    across = (((1,), (1,)), ((), ()))
    for at, piece in enumerate((pair_ref, far_ref)):
        rows = slice(at * half, (at + 1) * half)
        term = lax.dot_general(
            piece[0], wg_ref[...], across, preferred_element_type=jnp.float32
        ) + lax.dot_general(piece[1], wu_ref[...], across, preferred_element_type=jnp.float32)

        @pl.when(first)
        def _():
            out_ref[rows] = term + refs[0][rows] if started else term

        @pl.when(jnp.logical_not(first))
        def _():
            out_ref[rows] += term


def input_part(pair, far, wg, wu, held, start, width):
    half = pair.shape[1]
    depth = wg.shape[0]
    step = block_of(width)
    first = start // step
    started = held is not None
    piece = pl.BlockSpec((2, half, step), lambda j: (0, 0, j))
    columns = pl.BlockSpec((depth, step), lambda j: (0, first + j))
    total = pl.BlockSpec((2 * half, depth), lambda j: (0, 0), pipeline_mode=pl.Buffered(1))
    return pl.pallas_call(
        functools.partial(input_kernel, started),
        grid=(width // step,),
        in_specs=[piece, piece, columns, columns] + [total] * started,
        out_specs=pl.BlockSpec((2 * half, depth), lambda j: (0, 0)),
        out_shape=jax.ShapeDtypeStruct((2 * half, depth), jnp.float32),
        input_output_aliases={4: 0} if started else {},
        compiler_params=params(),
        cost_estimate=pl.CostEstimate(
            flops=8 * half * depth * width,
            bytes_accessed=8 * half * width + 4 * depth * width + 16 * half * depth,
            transcendentals=0,
        ),
        name="input_part",
    )(pair, far, wg, wu, *([held] if started else []))


def per_device(n_dp, n_row, n_col, codes, scales, pad_mask, cotangent, w_gate, w_up, w_out):
    row = lax.axis_index("row")
    depth, full = w_gate.shape
    near = [(r, r ^ 1) for r in range(n_row)]
    apart = [(r, r ^ 2) for r in range(n_row)]
    inward, outward, middle = [(0, 1), (3, 2)], [(1, 0), (2, 3)], [(1, 2), (2, 1)]
    across = [(d, d ^ 1) for d in range(n_dp)]

    stashed = unpack_stash(codes, scales)
    live_grad = (cotangent.astype(jnp.float32) * pad_mask.astype(jnp.float32)[:, None]).astype(
        jnp.bfloat16
    )
    mine = jnp.stack([stashed, live_grad])

    def spread(blocks):
        bit = n_col // 2
        held = {0: blocks}
        while bit:
            keys = sorted(held)
            packed = jnp.concatenate([held[k] for k in keys], axis=1)
            got = lax.ppermute(packed, "col", [(c, c ^ bit) for c in range(n_col)])
            for at, k in enumerate(keys):
                held[k ^ bit] = got[:, at * blocks.shape[1] : (at + 1) * blocks.shape[1]]
            bit //= 2
        return jnp.concatenate([held[k] for k in range(n_col)], axis=1)

    side = row // 2
    far_inner = jnp.where(side == 0, 2, 1)
    far_outer = jnp.where(side == 0, 3, 0)
    order = [row, row ^ 1, far_inner, far_outer]

    def arrange(gathered):
        unit = gathered.shape[1] // n_row
        return jnp.concatenate(
            [lax.dynamic_slice_in_dim(gathered, k * unit, unit, axis=1) for k in order], axis=1
        )

    both = arrange(spread(mine))
    x, g = both[0], both[1]
    tokens = x.shape[0]
    unit = tokens // n_row

    peaks = jnp.stack([jnp.max(jnp.abs(a)).astype(jnp.float32) for a in (w_gate, w_up, w_out, g)])
    for pairs in (near, apart):
        peaks = jnp.maximum(peaks, lax.ppermute(peaks, "row", pairs))
    lefts = jnp.stack([jnp.float32(stash_bound), jnp.float32(stash_bound), peaks[3]])
    bound = jnp.maximum(lefts * peaks[:3] * (depth * n_row), 1e-30)
    scale, inverse = half_range / bound, bound / half_range

    others = arrange(spread(lax.ppermute(mine, "dp", across)))
    turned = jnp.concatenate([both, others], axis=1).transpose(0, 2, 1)
    xt, gt = turned[0], turned[1]

    weights = (w_gate, w_up, w_out)
    portions = shares if full % (sum(shares) * lanes) == 0 else (1,)
    piece = full // sum(portions)
    starts, at = [], 0
    for share in portions:
        starts.append((at, share * piece))
        at += share * piece

    held, total = (), None
    for start, width in starts:
        p = project(scale, x, g, *weights, start, width)
        recv_a = lax.ppermute(p[:, 2 * unit :].astype(jnp.float16), "row", inward)
        send_c = (p[:, 2 * unit :] + recv_a.astype(jnp.float32)).astype(jnp.float16)
        recv_c = lax.ppermute(send_c, "row", middle)
        send_b = (p[:, unit : 2 * unit] + recv_c[:, unit:].astype(jnp.float32)).astype(jnp.float16)
        recv_b = lax.ppermute(send_b, "row", near)
        own = activate(inverse, p, recv_c, recv_b)

        pair = jnp.concatenate([own, lax.ppermute(own, "row", near)], axis=1)
        pair_x = lax.ppermute(pair, "dp", across)
        far_mid = lax.ppermute(pair, "row", middle)
        far = far_mid + lax.ppermute(far_mid, "row", outward)
        far_x = lax.ppermute(far, "dp", across)
        total = input_part(pair, far, w_gate, w_up, total, start, width)
        held = weight_grads(xt, gt, (pair, far, pair_x, far_x), held, start, width, full)

    spots = [
        jnp.where(row == k, 0, jnp.where(row ^ 1 == k, 1, 2 if k in (1, 2) else 3))
        for k in range(n_row)
    ]
    natural = jnp.concatenate(
        [lax.dynamic_slice_in_dim(total, s * unit, unit, axis=0) for s in spots], axis=0
    )
    block = codes.shape[0]
    parts = {k: natural[k * block : (k + 1) * block] for k in range(n_col)}
    bit = 1
    while bit < n_col:
        leaving = [k for k in sorted(parts) if k & bit]
        packed = jnp.concatenate([parts.pop(k) for k in leaving], axis=0)
        wire = packed.astype(jnp.float32 if bit == 1 else jnp.bfloat16)
        got = lax.ppermute(wire, "col", [(c, c ^ bit) for c in range(n_col)]).astype(jnp.float32)
        for i, k in enumerate(leaving):
            parts[k ^ bit] = parts[k ^ bit] + got[i * block : (i + 1) * block]
        bit *= 2
    return (parts[0], *held)


def solution(mesh):
    sizes = (mesh.shape["dp"], mesh.shape["row"], mesh.shape["col"])
    if sizes[0] != 2 or sizes[1] != 4:
        raise ValueError("unexpected mesh")
    return jax.shard_map(
        functools.partial(per_device, *sizes),
        mesh=mesh,
        in_specs=(
            P(("dp", "col"), "row"),
            P(("dp", "col"), "row"),
            P(("dp", "col")),
            P(("dp", "col"), "row"),
            P("row", "col"),
            P("row", "col"),
            P("row", "col"),
        ),
        out_specs=(P(("dp", "col"), "row"), P("row", "col"), P("row", "col"), P("row", "col")),
        check_vma=False,
    )
```

```python
import functools

import jax
import jax.numpy as jnp
from jax import lax
from jax.experimental import pallas as pl
from jax.experimental.pallas import tpu as pltpu
from jax.sharding import PartitionSpec as P


root_term = 0.7978845608028654
cubic_term = 0.044715
lanes = 128
stash_bound = 1.5
half_range = 32000.0
shares = (1, 1, 1, 2, 2, 1, 1, 1)


def gelu_pair(values):
    inside = root_term * (values + cubic_term * values * values * values)
    tangent = jnp.tanh(inside)
    activated = 0.5 * values * (1.0 + tangent)
    derivative = 0.5 * (1.0 + tangent) + 0.5 * values * (1.0 - tangent * tangent) * root_term * (
        1.0 + 3.0 * cubic_term * values * values
    )
    return (activated, derivative)


def unpack_kernel(codes_ref, scales_ref, mask_ref, cotangent_ref, out_ref, peak_ref):
    blocks = scales_ref.shape[1]
    width = codes_ref.shape[1] // blocks
    for at in range(blocks):
        columns = slice(at * width, (at + 1) * width)
        levels = (2 * codes_ref[:, columns] - 3).astype(jnp.float32)
        scaled = levels * scales_ref[:, at : at + 1].astype(jnp.float32) * (1.0 / 16.0)
        out_ref[0, :, columns] = scaled.astype(jnp.bfloat16)
    live = cotangent_ref[...].astype(jnp.float32) * mask_ref[...].astype(jnp.float32)
    out_ref[1] = live.astype(jnp.bfloat16)
    peak_ref[...] = fold(live)


def fold(values):
    rows, columns = values.shape
    tall = jnp.max(jnp.abs(values).reshape(rows // 8, 8, columns), axis=0)
    best = tall[:, :lanes]
    for at in range(1, columns // lanes):
        best = jnp.maximum(best, tall[:, at * lanes : (at + 1) * lanes])
    return best


def unpack(codes, scales, mask, cotangent):
    return pl.pallas_call(
        unpack_kernel,
        out_shape=[
            jax.ShapeDtypeStruct((2, *codes.shape), jnp.bfloat16),
            jax.ShapeDtypeStruct((8, lanes), jnp.float32),
        ],
        compiler_params=params(),
        cost_estimate=pl.CostEstimate(
            flops=8 * codes.size, bytes_accessed=10 * codes.size, transcendentals=0
        ),
        name="unpack",
    )(codes, scales, mask[:, None], cotangent)


def peaks_kernel(wg_ref, wu_ref, wo_ref, out_ref):
    first = pl.program_id(0) == 0
    for at, ref in enumerate((wg_ref, wu_ref, wo_ref)):
        best = fold(ref[...].astype(jnp.float32))
        out_ref[at] = jnp.maximum(best, jnp.where(first, 0.0, out_ref[at]))


def weight_peaks(*weights):
    depth, full = weights[0].shape
    rows = 64
    return pl.pallas_call(
        peaks_kernel,
        grid=(depth // rows,),
        in_specs=[pl.BlockSpec((rows, full), lambda i: (i, 0))] * 3,
        out_specs=pl.BlockSpec((3, 8, lanes), lambda i: (0, 0, 0)),
        out_shape=jax.ShapeDtypeStruct((3, 8, lanes), jnp.float32),
        compiler_params=params(),
        cost_estimate=pl.CostEstimate(
            flops=6 * depth * full, bytes_accessed=6 * depth * full, transcendentals=0
        ),
        name="weight_peaks",
    )(*weights)


def block_of(width):
    return 256 if width % 256 == 0 else lanes


def params(mib=48):
    return pltpu.CompilerParams(vmem_limit_bytes=mib * 1024 * 1024)


def project_kernel(both_ref, wg_ref, wu_ref, wo_ref, p_ref):
    for at, right in enumerate((wg_ref, wu_ref, wo_ref)):
        p_ref[at] = jnp.dot(both_ref[at // 2], right[...], preferred_element_type=jnp.float32)


def project(both, wg, wu, wo, start, width):
    _, tokens, depth = both.shape
    step = block_of(width)
    first = start // step
    whole = pl.BlockSpec(both.shape, lambda j: (0, 0, 0), pipeline_mode=pl.Buffered(1))
    columns = pl.BlockSpec((depth, step), lambda j: (0, first + j))
    return pl.pallas_call(
        project_kernel,
        grid=(width // step,),
        in_specs=[whole, columns, columns, columns],
        out_specs=pl.BlockSpec((3, tokens, step), lambda j: (0, 0, j)),
        out_shape=jax.ShapeDtypeStruct((3, tokens, width), jnp.float32),
        compiler_params=params(),
        cost_estimate=pl.CostEstimate(
            flops=6 * tokens * depth * width,
            bytes_accessed=4 * tokens * depth + 6 * depth * width + 12 * tokens * width,
            transcendentals=0,
        ),
        name="project",
    )(both, wg, wu, wo)


def activate(inverse, kept, arrived):
    gate_pre, up_part, back_grad = (
        kept.astype(jnp.float32) + arrived.astype(jnp.float32)
    ) * inverse
    activated, derivative = gelu_pair(gate_pre)
    return jnp.stack(
        [
            (back_grad * up_part * derivative).astype(jnp.bfloat16),
            (back_grad * activated).astype(jnp.bfloat16),
            (activated * up_part).astype(jnp.bfloat16),
        ]
    )


def weight_kernel(count, turned_ref, *refs):
    pieces, outs = refs[:count], refs[-3:]
    for at in range(3):
        left = turned_ref.at[at // 2]
        total, begin = None, 0
        for piece in pieces:
            rows = piece.shape[1]
            term = jnp.dot(
                left[:, begin : begin + rows], piece[at], preferred_element_type=jnp.float32
            )
            total = term if total is None else total + term
            begin += rows
        outs[at][...] = total


def weight_grads(turned, pieces, held, start, width, full):
    _, depth, tokens = turned.shape
    step = block_of(width)
    first = start // step
    count = len(pieces)
    whole = pl.BlockSpec(turned.shape, lambda j: (0, 0, 0), pipeline_mode=pl.Buffered(1))
    specs = [pl.BlockSpec((3, a.shape[1], step), lambda j: (0, 0, j)) for a in pieces]
    return pl.pallas_call(
        functools.partial(weight_kernel, count),
        grid=(width // step,),
        in_specs=[whole, *specs] + [pl.BlockSpec(memory_space=pl.ANY)] * len(held),
        out_specs=[pl.BlockSpec((depth, step), lambda j: (0, first + j))] * 3,
        out_shape=[jax.ShapeDtypeStruct((depth, full), jnp.float32)] * 3,
        input_output_aliases={1 + count + i: i for i in range(len(held))},
        compiler_params=params(),
        cost_estimate=pl.CostEstimate(
            flops=6 * tokens * depth * width,
            bytes_accessed=4 * tokens * depth + 6 * tokens * width + 12 * depth * width,
            transcendentals=0,
        ),
        name="weight_grads",
    )(turned, *pieces, *held)


def input_kernel(started, piece_ref, wg_ref, wu_ref, *refs):
    out_ref = refs[-1]
    first = pl.program_id(0) == 0
    across = (((1,), (1,)), ((), ()))
    term = lax.dot_general(
        piece_ref[0], wg_ref[...], across, preferred_element_type=jnp.float32
    ) + lax.dot_general(piece_ref[1], wu_ref[...], across, preferred_element_type=jnp.float32)

    @pl.when(first)
    def _():
        out_ref[...] = term + refs[0][...] if started else term

    @pl.when(jnp.logical_not(first))
    def _():
        out_ref[...] += term


def input_part(piece, wg, wu, held, start, width):
    tokens = piece.shape[1]
    depth = wg.shape[0]
    step = block_of(width)
    first = start // step
    started = held is not None
    columns = pl.BlockSpec((depth, step), lambda j: (0, first + j))
    total = pl.BlockSpec((tokens, depth), lambda j: (0, 0), pipeline_mode=pl.Buffered(1))
    return pl.pallas_call(
        functools.partial(input_kernel, started),
        grid=(width // step,),
        in_specs=[pl.BlockSpec((2, tokens, step), lambda j: (0, 0, j)), columns, columns]
        + [total] * started,
        out_specs=pl.BlockSpec((tokens, depth), lambda j: (0, 0)),
        out_shape=jax.ShapeDtypeStruct((tokens, depth), jnp.float32),
        input_output_aliases={3: 0} if started else {},
        compiler_params=params(),
        cost_estimate=pl.CostEstimate(
            flops=4 * tokens * depth * width,
            bytes_accessed=4 * tokens * width + 4 * depth * width + 8 * tokens * depth,
            transcendentals=0,
        ),
        name="input_part",
    )(piece, wg, wu, *([held] if started else []))


def after(value, earlier):
    return value if earlier is None else lax.optimization_barrier((value, earlier))[0]


def per_device(n_dp, n_row, n_col, codes, scales, pad_mask, cotangent, w_gate, w_up, w_out):
    return body(n_dp, n_row, n_col, codes, scales, pad_mask, cotangent, w_gate, w_up, w_out)


def body(n_dp, n_row, n_col, codes, scales, pad_mask, cotangent, w_gate, w_up, w_out):
    row = lax.axis_index("row")
    depth, full = w_gate.shape
    inward, outward, middle = [(0, 1), (3, 2)], [(1, 0), (2, 3)], [(1, 2), (2, 1)]
    across = [(d, d ^ 1) for d in range(n_dp)]

    def flip(bit, count):
        return [(k, k ^ bit) for k in range(count)]

    mine, grad_peak = unpack(codes, scales, pad_mask, cotangent)
    block = codes.shape[0]

    def spread(blocks):
        bit = n_col // 2
        held = {0: blocks}
        while bit:
            keys = sorted(held)
            packed = jnp.concatenate([held[k] for k in keys], axis=1)
            got = lax.ppermute(packed, "col", flip(bit, n_col))
            for at, k in enumerate(keys):
                held[k ^ bit] = got[:, at * block : (at + 1) * block]
            bit //= 2
        return jnp.concatenate([held[k] for k in range(n_col)], axis=1)

    both = spread(mine)

    peaks = jnp.concatenate([weight_peaks(w_gate, w_up, w_out), grad_peak[None]])
    for axis, count in (("row", n_row), ("col", n_col)):
        bit = 1
        while bit < count:
            peaks = jnp.maximum(peaks, lax.ppermute(peaks, axis, flip(bit, count)))
            bit *= 2
    peaks = jnp.max(peaks, axis=(1, 2), keepdims=True)
    lefts = jnp.concatenate([jnp.full((2, 1, 1), stash_bound, jnp.float32), peaks[3:]])
    bound = jnp.maximum(lefts * peaks[:3] * (depth * n_row), 1e-30)
    inner = (row == 1) | (row == 2)
    scale, inverse = half_range / bound, jnp.where(inner, bound / half_range, 0.0)

    others = spread(lax.ppermute(mine, "dp", across))
    turned = jnp.concatenate([both, others], axis=1).transpose(0, 2, 1)

    weights = (w_gate, w_up, w_out)
    portions = portions_of(full)
    piece = full // sum(portions)
    held, total, start, last = (), None, 0, {}
    for share in portions:
        width = share * piece
        p = project(both, *weights, start, width)
        scaled = after(p, last.get("a")) * scale
        last["a"] = scaled.astype(jnp.float16)
        recv_a = after(lax.ppermute(last["a"], "row", inward), last.get("c"))
        last["c"] = (scaled + recv_a.astype(jnp.float32)).astype(jnp.float16)
        arrived = after(lax.ppermute(last["c"], "row", middle), last.get("o"))
        last["o"] = activate(inverse, last["c"], arrived)
        back = after(lax.ppermute(last["o"], "row", outward), last.get("y"))
        ready = last["y"] = last["o"] + back
        other = lax.ppermute(ready, "dp", across)
        total = input_part(ready, w_gate, w_up, total, start, width)
        held = weight_grads(turned, (ready, other), held, start, width, full)
        start += width

    parts = {k: total[k * block : (k + 1) * block] for k in range(n_col)}
    bit = 1
    while bit < n_col:
        leaving = [k for k in sorted(parts) if k & bit]
        packed = jnp.concatenate([parts.pop(k) for k in leaving], axis=0)
        wire = packed.astype(jnp.float32 if bit == 1 else jnp.bfloat16)
        got = lax.ppermute(wire, "col", flip(bit, n_col)).astype(jnp.float32)
        for i, k in enumerate(leaving):
            parts[k ^ bit] = parts[k ^ bit] + got[i * block : (i + 1) * block]
        bit *= 2
    return (parts[0], *held)


def portions_of(full):
    return shares if full % (sum(shares) * lanes) == 0 else (1,)


def solution(mesh):
    sizes = (mesh.shape["dp"], mesh.shape["row"], mesh.shape["col"])
    if sizes[0] != 2 or sizes[1] != 4:
        raise ValueError("unexpected mesh")
    return jax.shard_map(
        functools.partial(per_device, *sizes),
        mesh=mesh,
        in_specs=(
            P(("dp", "col"), "row"),
            P(("dp", "col"), "row"),
            P(("dp", "col")),
            P(("dp", "col"), "row"),
            P("row", "col"),
            P("row", "col"),
            P("row", "col"),
        ),
        out_specs=(P(("dp", "col"), "row"), P("row", "col"), P("row", "col"), P("row", "col")),
        check_vma=False,
    )
```

```python
import functools

import jax
import jax.numpy as jnp
from jax import lax
from jax.experimental import pallas as pl
from jax.experimental.pallas import tpu as pltpu
from jax.sharding import PartitionSpec as P


root_term = 0.7978845608028654
cubic_term = 0.044715
lanes = 128
stash_bound = 1.5
half_range = 32000.0
stripe_rows = 512
most_tokens = 512
shares = (1, 2, 2, 2, 2, 1)


def gelu_pair(values):
    inside = root_term * (values + cubic_term * values * values * values)
    tangent = jnp.tanh(inside)
    activated = 0.5 * values * (1.0 + tangent)
    derivative = 0.5 * (1.0 + tangent) + 0.5 * values * (1.0 - tangent * tangent) * root_term * (
        1.0 + 3.0 * cubic_term * values * values
    )
    return (activated, derivative)


def unpack_kernel(codes_ref, scales_ref, mask_ref, cotangent_ref, out_ref, peak_ref):
    blocks = scales_ref.shape[1]
    width = codes_ref.shape[1] // blocks
    for at in range(blocks):
        columns = slice(at * width, (at + 1) * width)
        levels = (2 * codes_ref[:, columns] - 3).astype(jnp.float32)
        scaled = levels * scales_ref[:, at : at + 1].astype(jnp.float32) * (1.0 / 16.0)
        out_ref[0, :, columns] = scaled.astype(jnp.bfloat16)
    live = cotangent_ref[...].astype(jnp.float32) * mask_ref[...].astype(jnp.float32)
    out_ref[1] = live.astype(jnp.bfloat16)
    peak_ref[...] = fold(live)


def fold(values):
    rows, columns = values.shape
    tall = jnp.max(jnp.abs(values).reshape(rows // 8, 8, columns), axis=0)
    best = tall[:, :lanes]
    for at in range(1, columns // lanes):
        best = jnp.maximum(best, tall[:, at * lanes : (at + 1) * lanes])
    return best


def unpack(codes, scales, mask, cotangent):
    return pl.pallas_call(
        unpack_kernel,
        out_shape=[
            jax.ShapeDtypeStruct((2, *codes.shape), jnp.bfloat16),
            jax.ShapeDtypeStruct((8, lanes), jnp.float32),
        ],
        compiler_params=params(),
        cost_estimate=pl.CostEstimate(
            flops=8 * codes.size, bytes_accessed=10 * codes.size, transcendentals=0
        ),
        name="unpack",
    )(codes, scales, mask[:, None], cotangent)


def peaks_kernel(wg_ref, wu_ref, wo_ref, out_ref):
    first = pl.program_id(0) == 0
    for at, ref in enumerate((wg_ref, wu_ref, wo_ref)):
        best = fold(ref[...].astype(jnp.float32))
        out_ref[at] = jnp.maximum(best, jnp.where(first, 0.0, out_ref[at]))


def weight_peaks(*weights):
    depth, full = weights[0].shape
    rows = 64
    return pl.pallas_call(
        peaks_kernel,
        grid=(depth // rows,),
        in_specs=[pl.BlockSpec((rows, full), lambda i: (i, 0))] * 3,
        out_specs=pl.BlockSpec((3, 8, lanes), lambda i: (0, 0, 0)),
        out_shape=jax.ShapeDtypeStruct((3, 8, lanes), jnp.float32),
        compiler_params=params(),
        cost_estimate=pl.CostEstimate(
            flops=6 * depth * full, bytes_accessed=6 * depth * full, transcendentals=0
        ),
        name="weight_peaks",
    )(*weights)


def block_of(width):
    return 256 if width % 256 == 0 else lanes


def params(mib=24):
    return pltpu.CompilerParams(vmem_limit_bytes=mib * 1024 * 1024)


def project_kernel(both_ref, wg_ref, wu_ref, wo_ref, p_ref):
    for at, right in enumerate((wg_ref, wu_ref, wo_ref)):
        p_ref[at] = jnp.dot(both_ref[at // 2], right[...], preferred_element_type=jnp.float32)


def project(both, wg, wu, wo, start, width):
    _, tokens, depth = both.shape
    step = block_of(width)
    first = start // step
    whole = pl.BlockSpec(both.shape, lambda j: (0, 0, 0), pipeline_mode=pl.Buffered(1))
    columns = pl.BlockSpec((depth, step), lambda j: (0, first + j))
    return pl.pallas_call(
        project_kernel,
        grid=(width // step,),
        in_specs=[whole, columns, columns, columns],
        out_specs=pl.BlockSpec((3, tokens, step), lambda j: (0, 0, j)),
        out_shape=jax.ShapeDtypeStruct((3, tokens, width), jnp.float32),
        compiler_params=params(),
        cost_estimate=pl.CostEstimate(
            flops=6 * tokens * depth * width,
            bytes_accessed=4 * tokens * depth + 6 * depth * width + 12 * tokens * width,
            transcendentals=0,
        ),
        name="project",
    )(both, wg, wu, wo)


def activate(inverse, kept, arrived):
    gate_pre, up_part, back_grad = (
        kept.astype(jnp.float32) + arrived.astype(jnp.float32)
    ) * inverse
    activated, derivative = gelu_pair(gate_pre)
    return jnp.stack(
        [
            (back_grad * up_part * derivative).astype(jnp.bfloat16),
            (back_grad * activated).astype(jnp.bfloat16),
            (activated * up_part).astype(jnp.bfloat16),
        ]
    )


def weight_kernel(count, first, turn_ref, *refs):
    lefts, pieces = refs[:count], refs[count : 2 * count]
    earlier, outs = refs[2 * count : 2 * count + 3], refs[2 * count + 3 : 2 * count + 6]
    kept, sem = refs[-2:]
    step = outs[0].shape[1]

    def stripe(at_row, carry):
        rows = pl.ds(pl.multiple_of(at_row * stripe_rows, stripe_rows), stripe_rows)
        for at in range(3):
            outs[at][rows, :] = sum(
                jnp.dot(left[at // 2, rows, :], piece[at], preferred_element_type=jnp.float32)
                for left, piece in zip(lefts, pieces)
            )
        return carry

    lax.fori_loop(0, outs[0].shape[0] // stripe_rows, stripe, 0)

    @pl.when(turn_ref[0] > 0)
    def _():
        begin = pl.multiple_of((first + pl.program_id(0)) * step, step)
        for at in range(3):
            copy = pltpu.make_async_copy(earlier[at].at[:, pl.ds(begin, step)], kept, sem)
            copy.start()
            copy.wait()
            outs[at][...] += kept[...]


def weight_grads(turn, lefts, pieces, held, start, width):
    _, depth, tokens = lefts[0].shape
    step = block_of(width)
    first = start // step
    count = len(pieces)
    whole = [
        pl.BlockSpec(a.shape, lambda j: (0, 0, 0), pipeline_mode=pl.Buffered(1)) for a in lefts
    ]
    specs = [pl.BlockSpec((3, tokens, step), lambda j: (0, 0, j))] * count
    return pl.pallas_call(
        functools.partial(weight_kernel, count, first),
        grid=(width // step,),
        in_specs=[pl.BlockSpec(memory_space=pltpu.SMEM), *whole, *specs]
        + [pl.BlockSpec(memory_space=pl.ANY)] * 3,
        out_specs=[pl.BlockSpec((depth, step), lambda j: (0, first + j))] * 3,
        out_shape=[jax.ShapeDtypeStruct(a.shape, a.dtype) for a in held],
        input_output_aliases={1 + 2 * count + i: i for i in range(3)},
        scratch_shapes=[pltpu.VMEM((depth, step), jnp.float32), pltpu.SemaphoreType.DMA],
        compiler_params=params(),
        cost_estimate=pl.CostEstimate(
            flops=6 * count * tokens * depth * width,
            bytes_accessed=count * tokens * (4 * depth + 6 * width) + 12 * depth * width,
            transcendentals=0,
        ),
        name="weight_grads",
    )(turn, *lefts, *pieces, *held)


def blank(depth, full):
    return pl.pallas_call(
        lambda *outs: None,
        out_specs=[pl.BlockSpec(memory_space=pl.ANY)] * 3,
        out_shape=[jax.ShapeDtypeStruct((depth, full), jnp.float32)] * 3,
        name="blank",
    )()


def input_kernel(started, piece_ref, wg_ref, wu_ref, *refs):
    out_ref = refs[-1]
    first = pl.program_id(0) == 0
    across = (((1,), (1,)), ((), ()))

    @pl.when(first)
    def _():
        out_ref[...] = refs[0][...] if started else jnp.zeros_like(out_ref)

    def stripe(at_row, carry):
        rows = pl.ds(pl.multiple_of(at_row * stripe_rows, stripe_rows), stripe_rows)
        out_ref[:, rows] += lax.dot_general(
            piece_ref[0], wg_ref[rows, :], across, preferred_element_type=jnp.float32
        ) + lax.dot_general(
            piece_ref[1], wu_ref[rows, :], across, preferred_element_type=jnp.float32
        )
        return carry

    lax.fori_loop(0, wg_ref.shape[0] // stripe_rows, stripe, 0)


def input_part(piece, wg, wu, held, start, width):
    tokens = piece.shape[1]
    depth = wg.shape[0]
    step = block_of(width)
    first = start // step
    started = held is not None
    columns = pl.BlockSpec((depth, step), lambda j: (0, first + j))
    total = pl.BlockSpec((tokens, depth), lambda j: (0, 0), pipeline_mode=pl.Buffered(1))
    return pl.pallas_call(
        functools.partial(input_kernel, started),
        grid=(width // step,),
        in_specs=[pl.BlockSpec((2, tokens, step), lambda j: (0, 0, j)), columns, columns]
        + [total] * started,
        out_specs=pl.BlockSpec((tokens, depth), lambda j: (0, 0)),
        out_shape=jax.ShapeDtypeStruct((tokens, depth), jnp.float32),
        input_output_aliases={3: 0} if started else {},
        compiler_params=params(),
        cost_estimate=pl.CostEstimate(
            flops=4 * tokens * depth * width,
            bytes_accessed=4 * tokens * width + 4 * depth * width + 8 * tokens * depth,
            transcendentals=0,
        ),
        name="input_part",
    )(piece, wg, wu, *([held] if started else []))


def slots_of(turn_ref, mask_ref, capacity):
    blocks, width = mask_ref.shape
    live = mask_ref[...]
    before = lax.broadcasted_iota(jnp.int32, (width, width), 0)
    at = lax.broadcasted_iota(jnp.int32, (width, width), 1)
    upto = jnp.dot(
        live, (before <= at).astype(jnp.float32), preferred_element_type=jnp.float32
    )
    slot = lax.broadcasted_iota(jnp.int32, (capacity, width), 0).astype(jnp.float32)
    skipped = (turn_ref[0] * capacity).astype(jnp.float32)
    picks, passed = [], jnp.zeros((1, 1), jnp.float32) - skipped
    for k in range(blocks):
        spot = upto[k : k + 1] - 1.0 + passed
        picks.append(jnp.where((slot == spot) & (live[k : k + 1] > 0.5), 1.0, 0.0))
        passed = passed + upto[k : k + 1, width - 1 :]
    return jnp.concatenate(picks, axis=1)


def pack_kernel(turn_ref, mask_ref, *refs):
    pieces, out_ref = refs[:-1], refs[-1]
    picks = slots_of(turn_ref, mask_ref, out_ref.shape[1]).astype(jnp.bfloat16)
    for at in range(2):
        total, begin = None, 0
        for piece in pieces:
            rows = piece.shape[1]
            term = jnp.dot(
                picks[:, begin : begin + rows], piece[at], preferred_element_type=jnp.float32
            )
            total = term if total is None else total + term
            begin += rows
        out_ref[at] = total.astype(jnp.bfloat16)


def pack(turn, mask, pieces, capacity):
    depth = pieces[0].shape[2]
    return pl.pallas_call(
        pack_kernel,
        in_specs=[pl.BlockSpec(memory_space=pltpu.SMEM)]
        + [pl.BlockSpec(memory_space=pltpu.VMEM)] * (1 + len(pieces)),
        out_shape=jax.ShapeDtypeStruct((2, capacity, depth), jnp.bfloat16),
        compiler_params=params(),
        cost_estimate=pl.CostEstimate(
            flops=4 * capacity * mask.size * depth,
            bytes_accessed=4 * (capacity + mask.size) * depth,
            transcendentals=0,
        ),
        name="pack",
    )(turn, mask, *pieces)


def unpack_rows_kernel(turn_ref, mask_ref, packed_ref, out_ref):
    picks = slots_of(turn_ref, mask_ref, packed_ref.shape[0]).astype(jnp.bfloat16)
    values = packed_ref[...]
    high = values.astype(jnp.bfloat16)
    rest = values - high.astype(jnp.float32)
    middle = rest.astype(jnp.bfloat16)
    low = (rest - middle.astype(jnp.float32)).astype(jnp.bfloat16)
    down = (((0,), (0,)), ((), ()))
    out_ref[...] = sum(
        lax.dot_general(picks, part, down, preferred_element_type=jnp.float32)
        for part in (low, middle, high)
    )


def unpack_rows(turn, mask, packed):
    depth = packed.shape[1]
    return pl.pallas_call(
        unpack_rows_kernel,
        in_specs=[pl.BlockSpec(memory_space=pltpu.SMEM)]
        + [pl.BlockSpec(memory_space=pltpu.VMEM)] * 2,
        out_shape=jax.ShapeDtypeStruct((mask.size, depth), jnp.float32),
        compiler_params=params(),
        cost_estimate=pl.CostEstimate(
            flops=6 * packed.size * mask.size,
            bytes_accessed=4 * packed.size + 4 * mask.size * depth,
            transcendentals=0,
        ),
        name="unpack_rows",
    )(turn, mask, packed)


def after(value, earlier):
    return value if earlier is None else lax.optimization_barrier((value, earlier))[0]


def per_device(n_dp, n_row, n_col, codes, scales, pad_mask, cotangent, w_gate, w_up, w_out):
    return body(n_dp, n_row, n_col, codes, scales, pad_mask, cotangent, w_gate, w_up, w_out)


def flip(bit, count):
    return [(k, k ^ bit) for k in range(count)]


def spread(mine, count):
    pieces, keys, bit = [mine], [0], count // 2
    while bit:
        packed = pieces[0] if len(pieces) == 1 else jnp.concatenate(pieces, axis=1)
        pieces.append(lax.ppermute(packed, "col", flip(bit, count)))
        keys += [k ^ bit for k in keys]
        bit //= 2
    return pieces, keys


def top(values, axis, count, limit=None):
    bit = 1
    while bit < (limit or count):
        values = jnp.maximum(values, lax.ppermute(values, axis, flip(bit, count)))
        bit *= 2
    return values


def body(n_dp, n_row, n_col, codes, scales, pad_mask, cotangent, w_gate, w_up, w_out):
    sizes = (n_dp, n_row, n_col)
    group, col = lax.axis_index("dp"), lax.axis_index("col")
    block = codes.shape[0]
    tokens = n_col * block

    mine, grad_peak = unpack(codes, scales, pad_mask, cotangent)
    pieces, keys = spread(mine, n_col)

    own = lax.broadcasted_iota(jnp.int32, (n_dp * n_col, 1), 0) == group * n_col + col
    known = jnp.where(own, pad_mask.astype(jnp.float32)[None, :], 0.0)
    shared = jnp.concatenate([grad_peak[None], known.reshape(-1, 8, lanes)])
    shared = top(shared, "col", n_col)
    peaks = jnp.concatenate([weight_peaks(w_gate, w_up, w_out), shared[:1]])
    peaks = top(peaks, "row", n_row, n_row // 2)
    known = top(shared[1:], "dp", n_dp).reshape(n_dp, n_col, block)
    most = jnp.max(jnp.sum(known, axis=(1, 2)))

    def mask_of(which):
        plane = lax.dynamic_index_in_dim(known, which, 0, keepdims=False)
        return jnp.concatenate(
            [lax.dynamic_slice_in_dim(plane, col ^ k, 1, axis=0) for k in keys], axis=0
        )

    capacity = min(tokens, most_tokens) * 13 // 16
    passes = jnp.maximum((most.astype(jnp.int32) + capacity - 1) // capacity, 1)
    operands = (tuple(pieces), mine, (mask_of(group), mask_of(group ^ 1)), peaks)
    operands += (w_gate, w_up, w_out)
    one_pass = functools.partial(run, sizes, keys, capacity, operands)
    begin = (jnp.zeros(mine.shape[1:], jnp.float32), *blank(*w_gate.shape))
    return lax.fori_loop(0, passes, one_pass, begin)


def run(sizes, keys, capacity, operands, index, grads):
    pieces, mine, masks, peaks, w_gate, w_up, w_out = operands
    n_dp, n_row, n_col = sizes
    mine, peaks, index = lax.optimization_barrier((mine, peaks, index))
    turn = index.reshape(1)
    row = lax.axis_index("row")
    depth, full = w_gate.shape
    block = mine.shape[1]
    inward, outward, middle = [(0, 1), (3, 2)], [(1, 0), (2, 3)], [(1, 2), (2, 1)]
    across = flip(1, n_dp)

    half = n_row // 2
    peaks = jnp.maximum(peaks, lax.ppermute(peaks, "row", flip(half, n_row)))
    peaks = jnp.max(peaks, axis=(1, 2), keepdims=True)
    lefts = jnp.concatenate([jnp.full((2, 1, 1), stash_bound, jnp.float32), peaks[3:]])
    bound = jnp.maximum(lefts * peaks[:3] * (depth * n_row), 1e-30)
    inner = (row == 1) | (row == 2)
    scale, inverse = half_range / bound, jnp.where(inner, bound / half_range, 0.0)

    both = pack(turn, masks[0], pieces, capacity)
    theirs, _ = spread(lax.ppermute(mine, "dp", across), n_col)
    lefts = [a.transpose(0, 2, 1) for a in (both, pack(turn, masks[1], theirs, capacity))]

    weights = (w_gate, w_up, w_out)
    portions = portions_of(full)
    piece = full // sum(portions)
    (given, *held), total, start, last = grads, None, 0, {}
    for share in portions:
        width = share * piece
        p = project(both, *weights, start, width)
        scaled = after(p, last.get("a")) * scale
        last["a"] = scaled.astype(jnp.float16)
        recv_a = after(lax.ppermute(last["a"], "row", inward), last.get("c"))
        last["c"] = (scaled + recv_a.astype(jnp.float32)).astype(jnp.float16)
        arrived = after(lax.ppermute(last["c"], "row", middle), last.get("o"))
        last["o"] = activate(inverse, last["c"], arrived)
        back = after(lax.ppermute(last["o"], "row", outward), last.get("y"))
        ready = last["y"] = last["o"] + back
        other = lax.ppermute(ready, "dp", across)
        total = input_part(ready, w_gate, w_up, total, start, width)
        held = weight_grads(turn, lefts, (ready, other), held, start, width)
        start += width

    whole = unpack_rows(turn, masks[0], total)
    parts = {k: whole[i * block : (i + 1) * block] for i, k in enumerate(keys)}
    bit = 1
    while bit < n_col:
        leaving = [k for k in sorted(parts) if k & bit]
        packed = jnp.concatenate([parts.pop(k) for k in leaving], axis=0)
        wire = packed.astype(jnp.float32 if bit == 1 else jnp.bfloat16)
        got = lax.ppermute(wire, "col", flip(bit, n_col)).astype(jnp.float32)
        for i, k in enumerate(leaving):
            parts[k ^ bit] = parts[k ^ bit] + got[i * block : (i + 1) * block]
        bit *= 2
    return (given + parts[0], *held)


def portions_of(full):
    return shares if full % (sum(shares) * lanes) == 0 else (1,)


def solution(mesh):
    sizes = (mesh.shape["dp"], mesh.shape["row"], mesh.shape["col"])
    if sizes[0] != 2 or sizes[1] != 4:
        raise ValueError("unexpected mesh")
    return jax.shard_map(
        functools.partial(per_device, *sizes),
        mesh=mesh,
        in_specs=(
            P(("dp", "col"), "row"),
            P(("dp", "col"), "row"),
            P(("dp", "col")),
            P(("dp", "col"), "row"),
            P("row", "col"),
            P("row", "col"),
            P("row", "col"),
        ),
        out_specs=(P(("dp", "col"), "row"), P("row", "col"), P("row", "col"), P("row", "col")),
        check_vma=False,
    )
```
